32 devices in a mesh: groups: 2 (over y), tok: 4 (over z), ch: 2 (over x), sub: 2 (over core).
Axes of the slice: x: 2, y: 2, z: 4, core: 2. Of those that a mesh axis runs over, the one named last changes fastest.
Arguments:
- weather: float32 [128, 128, 128], P('groups', 'tok', ('ch', 'sub')), parts along dimension 0, may hold values from -6 to 6
- conv_first: float32 [9, 64, 64], replicated, may hold values from -0.25 to 0.25
- conv_second: float32 [9, 64, 64], replicated, may hold values from -0.25 to 0.25
- patch_embed: bfloat16 [256, 384], replicated, may hold values from -0.375 to 0.375
- token_mixing: bfloat16 [4096, 16384], P('tok', ('ch', 'sub')), may hold values from -0.09375 to 0.09375
Outputs:
- lifted: bfloat16 [768, 16384], P(('groups', 'tok'), ('ch', 'sub')), parts along dimension 0
The draws below stay inside these ranges and needn't reach their ends.
There are 2 independent parts, one for each index of `groups`. The reference program is written for one: setup_inputs(seed, part) draws one part's arguments, and reference() takes and returns one part's arrays. A program takes and returns all parts, laid end to end along the dimension named above; an argument that names none is the same for every part. Nothing has to cross between parts.
All inputs are finite; a program needn't handle non-finite values.
Results may differ from the reference program's by a relative error of at most 0.0058.
Values may be sent and summed in bfloat16 or wider, within the bound.
A program may use at most 64 MiB of HBM per device.

```python
import jax
import jax.numpy as jnp
from jax import lax

CIN = 64
EMBED = 384
HIDDEN_SIZE = 16384
LON = 128
LAT = 128
TOKENS = 4096
BAND = 1024
N_TOK = 4


def block_levels(rng, dims, pieces, smallest, high):
    gain, own = 1.0, jax.random.fold_in(rng, 6)
    for position, blocks in pieces:
        draws = jnp.exp(jax.random.uniform(jax.random.fold_in(own, position), (blocks,), jnp.float32, smallest / len(pieces), high / len(pieces)))
        gain = gain * jnp.repeat(draws, dims[position] // blocks).reshape([-1 if axis == position else 1 for axis in range(len(dims))])
    return gain


def normal_values(own_key, shape, deviation, limit, cuts=(), held_as=jnp.bfloat16):
    entries = jax.random.normal(own_key, shape, jnp.float32) * deviation
    if len(cuts) > 0:
        entries = block_levels(own_key, shape, cuts, -0.22, 0.18) * entries
    return jnp.clip(entries, min=-limit, max=limit).astype(held_as)


def setup_inputs(seed: int = 0, part: int = 0) -> dict:
    key_list = jax.random.split(jax.random.key(seed), 6)
    part_splits = jax.random.split(jax.random.fold_in(key_list[5], part), 6)
    return {
        "weather": normal_values(part_splits[0], (CIN, LON, LAT), 1.0, 6.0, ((1, 4), (2, 4)), jnp.float32),
        "conv_first": normal_values(key_list[1], (9, CIN, CIN), (9 * CIN) ** -0.5, 0.25, (), jnp.float32),
        "conv_second": normal_values(key_list[2], (9, CIN, CIN), (9 * CIN) ** -0.5, 0.25, (), jnp.float32),
        "patch_embed": normal_values(key_list[3], (4 * CIN, EMBED), (4 * CIN) ** -0.5, 0.375),
        "token_mixing": normal_values(key_list[4], (TOKENS, HIDDEN_SIZE), TOKENS ** -0.5, 0.09375, ((0, 4), (1, 4))),
    }


def convolve(field_in, kernel):
    width_lon = field_in.shape[1]
    width_lat = field_in.shape[2]
    looped = jnp.concatenate([field_in[:, -1:, :], field_in, field_in[:, :1, :]], axis=1)
    padded = jnp.pad(looped, ((0, 0), (0, 0), (1, 1)))
    summed = jnp.zeros((kernel.shape[1], width_lon, width_lat), jnp.float32)
    for row_shift in range(3):
        for col_shift in range(3):
            window = padded[:, row_shift:row_shift + width_lon, col_shift:col_shift + width_lat]
            summed = summed + jnp.einsum("oi,ixy->oxy", kernel[3 * row_shift + col_shift], window, precision=lax.Precision.HIGHEST)
    return summed


def reference(weather, conv_first, conv_second, patch_embed, token_mixing):
    hidden_one = jax.nn.gelu(convolve(weather, conv_first), approximate=False)
    field_two = convolve(hidden_one, conv_second).astype(jnp.bfloat16)
    blocks = field_two.reshape(CIN, LON // 2, 2, LAT // 2, 2).astype(jnp.float32)
    embed_four = patch_embed.reshape(CIN, 2, 2, EMBED).astype(jnp.float32)
    tokens = jnp.einsum("cpaqb,cabo->pqo", blocks, embed_four).reshape(TOKENS, EMBED).astype(jnp.bfloat16)
    token_blocks = tokens.reshape(N_TOK, BAND, EMBED)
    weight_blocks = token_mixing.reshape(N_TOK, BAND, HIDDEN_SIZE)

    def add_block(carry, pair):
        product = lax.dot_general(pair[0].astype(jnp.float32), pair[1].astype(jnp.float32), (((0,), (0,)), ((), ())))
        return carry + product, None

    summed, unused = lax.scan(add_block, jnp.zeros((EMBED, HIDDEN_SIZE), jnp.float32), (token_blocks, weight_blocks))
    return jax.nn.gelu(summed, approximate=False).astype(jnp.bfloat16)
```

```python
import functools

import jax
import jax.numpy as jnp
from jax import lax
from jax.experimental import pallas as pl
from jax.experimental.pallas import tpu as pltpu
from jax.sharding import PartitionSpec as P

MESH = pl.DeviceIdType.MESH
CHUNKS = 8
PIECES = 2


def padded_2(block, sides, width, periodic):
    for axis, dim in sides:
        count = lax.axis_size(axis)
        forward = [(i, i + 1) for i in range(count - 1)]
        if periodic:
            forward.append((count - 1, 0))
        backward = [(target, source) for source, target in forward]
        low = lax.ppermute(
            lax.slice_in_dim(block, block.shape[dim] - width, None, axis=dim), axis, forward
        )
        high = lax.ppermute(lax.slice_in_dim(block, 0, width, axis=dim), axis, backward)
        block = jnp.concatenate([low, block, high], axis=dim)
    return block


def valid_conv(padded, kernel):
    width_lon = padded.shape[1] - 2
    width_lat = padded.shape[2] - 2
    stacked = jnp.stack(
        [
            padded[:, row_shift : row_shift + width_lon, col_shift : col_shift + width_lat]
            for row_shift in range(3)
            for col_shift in range(3)
        ],
        0,
    )
    return jnp.einsum("toi,tixy->oxy", kernel, stacked, precision=lax.Precision.HIGHEST)


def embed_patches(field_in, patch_embed):
    chans, width_lon, width_lat = field_in.shape
    blocks = field_in.reshape(chans, width_lon // 2, 2, width_lat // 2, 2)
    embed_four = patch_embed.reshape(chans, 2, 2, patch_embed.shape[1])
    return jnp.einsum(
        "cpaqb,cabo->pqo", blocks, embed_four, preferred_element_type=jnp.float32
    ).astype(jnp.bfloat16)


def gelu_exact(v):
    return 0.5 * v * (1.0 + lax.erf(v * 0.7071067811865476))


def lift_kernel(
    n, tok_ref, w_ref, out_ref, tg, tt, wv, part, s_r, s_l, r_r, r_l,
    w_sem, ga_s, ga_r, gb_s, gb_r, gf_s, gf_r, rs_s, rs_r, ls_s, ls_r,
):
    z, x, s = lax.axis_index("tok"), lax.axis_index("ch"), lax.axis_index("sub")
    chunks, _, ob, hc = s_r.shape
    pieces = ga_s.shape[0]

    def w_copy(c):
        return pltpu.make_async_copy(
            w_ref.at[:, pl.ds(pl.multiple_of(c * hc, hc), hc)], wv.at[c], w_sem.at[c]
        )

    for c in range(chunks):
        w_copy(c).start()

    barrier = pltpu.get_barrier_semaphore()
    pl.semaphore_signal(barrier, inc=1, device_id={"ch": 1 - x}, device_id_type=MESH)
    pl.semaphore_signal(barrier, inc=1, device_id={"sub": 1 - s}, device_id_type=MESH)

    for peer in (lax.rem(z + 1, n), lax.rem(z + n - 1, n)):
        pl.semaphore_signal(barrier, inc=1, device_id={"tok": peer}, device_id_type=MESH)
    pl.semaphore_wait(barrier, 4)

    rows = tok_ref.shape[0]
    step = rows // pieces
    dev = x * 2 + s
    cross = (1 - x) * 2 + s
    copies = []
    for g in range(pieces):
        part_rows = pl.ds(g * step, step)
        copies.append((
            pltpu.make_async_remote_copy(
                tok_ref.at[part_rows], tg.at[part_rows, dev], gb_s.at[g], gb_r.at[g],
                device_id={"ch": 1 - x}, device_id_type=MESH),
            pltpu.make_async_remote_copy(
                tok_ref.at[part_rows], tg.at[part_rows, dev], ga_s.at[g], ga_r.at[g],
                device_id={"sub": 1 - s}, device_id_type=MESH),
            pltpu.make_async_remote_copy(
                tg.at[part_rows, cross], tg.at[part_rows, cross], gf_s.at[g], gf_r.at[g],
                device_id={"sub": 1 - s}, device_id_type=MESH),
        ))
    for over_x, over_s, _ in copies:
        over_x.start()
        over_s.start()
    tg[:, dev] = tok_ref[...]
    for over_x, _, onward in copies:
        over_x.wait_recv()
        onward.start()
    for over_x, over_s, onward in copies:
        over_s.wait_recv()
        onward.wait_recv()
        over_x.wait_send()
        over_s.wait_send()
        onward.wait_send()
    flat = tg[...].reshape(tt.shape[1], tt.shape[0])
    tt[...] = jnp.transpose(flat)

    def right_copy(c, d):
        return pltpu.make_async_remote_copy(
            s_r.at[c, d], r_r.at[c, d], rs_s.at[c, d], rs_r.at[c, d],
            device_id={"tok": z + 1}, device_id_type=MESH)

    def left_copy(c, d):
        return pltpu.make_async_remote_copy(
            s_l.at[c, d], r_l.at[c, d], ls_s.at[c, d], ls_r.at[c, d],
            device_id={"tok": z - 1}, device_id_type=MESH)

    def compute(c, carry):
        w_copy(c).wait()
        product = jnp.dot(tt[...], wv[c], preferred_element_type=jnp.float32)
        part[c] = product.reshape(n, ob, hc)

        @pl.when(z == 0)
        def _():
            for d in range(n - 1, 0, -1):
                s_r[c, d] = part[c, d].astype(jnp.bfloat16)
                right_copy(c, d).start()

        @pl.when(z == n - 1)
        def _():
            for d in range(n - 1):
                s_l[c, d] = part[c, d].astype(jnp.bfloat16)
                left_copy(c, d).start()

        return carry

    lax.fori_loop(0, chunks, compute, 0)

    def forward(c, carry):
        for d in range(n - 1, 0, -1):
            @pl.when((z > 0) & (z < d))
            def _():
                right_copy(c, d).wait_recv()
                s_r[c, d] = (part[c, d] + r_r[c, d].astype(jnp.float32)).astype(jnp.bfloat16)
                right_copy(c, d).start()

        for d in range(n - 1):
            @pl.when((z < n - 1) & (z > d))
            def _():
                left_copy(c, d).wait_recv()
                s_l[c, d] = (part[c, d] + r_l[c, d].astype(jnp.float32)).astype(jnp.bfloat16)
                left_copy(c, d).start()

        for d in range(n):
            @pl.when(z == d)
            def _():
                total = part[c, d]
                if d > 0:
                    right_copy(c, d).wait_recv()
                    total = total + r_r[c, d].astype(jnp.float32)
                if d < n - 1:
                    left_copy(c, d).wait_recv()
                    total = total + r_l[c, d].astype(jnp.float32)
                out_ref[:, pl.ds(pl.multiple_of(c * hc, hc), hc)] = gelu_exact(total).astype(out_ref.dtype)

        return carry

    lax.fori_loop(0, chunks, forward, 0)

    def drain(c, carry):
        for d in range(n):
            @pl.when(z < d)
            def _():
                right_copy(c, d).wait_send()

            @pl.when(z > d)
            def _():
                left_copy(c, d).wait_send()

        return carry

    lax.fori_loop(0, chunks, drain, 0)


def lift(local_tokens, token_mixing):
    n = lax.axis_size("tok")
    rows, width, embed = local_tokens.shape
    depth, cols = token_mixing.shape
    hc = cols // CHUNKS
    ob = embed // n
    dma, bf16 = pltpu.SemaphoreType.DMA, jnp.bfloat16
    blocks = pltpu.VMEM((CHUNKS, n, ob, hc), bf16)
    return pl.pallas_call(
        functools.partial(lift_kernel, n),
        out_shape=jax.ShapeDtypeStruct((ob, cols), bf16),
        in_specs=[pl.BlockSpec(memory_space=pltpu.VMEM), pl.BlockSpec(memory_space=pl.ANY)],
        out_specs=pl.BlockSpec(memory_space=pltpu.VMEM),
        scratch_shapes=[
            pltpu.VMEM((rows, 4, width, embed), bf16),
            pltpu.VMEM((embed, depth), bf16),
            pltpu.VMEM((CHUNKS, depth, hc), bf16),
            pltpu.VMEM((CHUNKS, n, ob, hc), jnp.float32),
            blocks, blocks, blocks, blocks,
            dma((CHUNKS,)),
        ] + [dma((PIECES,))] * 6 + [dma((CHUNKS, n))] * 4,
        compiler_params=pltpu.CompilerParams(
            collective_id=0, has_side_effects=True, vmem_limit_bytes=60 * 1024 * 1024
        ),
    )(local_tokens, token_mixing)


def fits(token_mixing, embed):
    n = lax.axis_size("tok")
    return (
        lax.axis_size("ch") == 2
        and lax.axis_size("sub") == 2
        and 1 < n <= 8
        and embed % (16 * n) == 0
        and token_mixing.shape[1] % (128 * CHUNKS) == 0
    )


def local(weather, conv_first, conv_second, patch_embed, token_mixing):
    widened = padded_2(weather, (("tok", 1),), 2, True)
    padded = padded_2(widened, ((("ch", "sub"), 2),), 2, False)
    hidden_one = jax.nn.gelu(valid_conv(padded, conv_first), approximate=False)
    width_lat = weather.shape[2]
    lat_index = (
        jnp.arange(width_lat + 2, dtype=jnp.int32) - 1 + lax.axis_index(("ch", "sub")) * width_lat
    )
    inside = (lat_index >= 0) & (lat_index < width_lat * lax.axis_size(("ch", "sub")))
    hidden_one = jnp.where(inside[None, None, :], hidden_one, jnp.float32(0.0))
    field_two = valid_conv(hidden_one, conv_second)
    field_two = field_two.astype(jnp.bfloat16)
    local_tokens = embed_patches(field_two, patch_embed)
    if fits(token_mixing, patch_embed.shape[1]):
        return lift(local_tokens, token_mixing)
    gathered = lax.all_gather(local_tokens, ("ch", "sub"), axis=1, tiled=True)
    tokens = gathered.reshape(-1, gathered.shape[2])
    summed = lax.psum_scatter(
        lax.dot_general(
            tokens, token_mixing, (((0,), (0,)), ((), ())), preferred_element_type=jnp.float32
        ),
        "tok",
        scatter_dimension=0,
        tiled=True,
    )
    return jax.nn.gelu(summed, approximate=False).astype(jnp.bfloat16)


def solution(mesh):
    placed = (P("groups", "tok", ("ch", "sub")), P(), P(), P(), P("tok", ("ch", "sub")))
    return jax.shard_map(
        local,
        mesh=mesh,
        in_specs=placed,
        out_specs=P(("groups", "tok"), ("ch", "sub")),
        check_vma=False,
    )
```

```python
import functools

import jax
import jax.numpy as jnp
from jax import lax
from jax.experimental import pallas as pl
from jax.experimental.pallas import tpu as pltpu
from jax.sharding import PartitionSpec as P

MESH = pl.DeviceIdType.MESH
CHUNKS = 8
PIECES = 2
LAG = 1


def padded_2(block, sides, width, periodic):
    for axis, dim in sides:
        count = lax.axis_size(axis)
        forward = [(i, i + 1) for i in range(count - 1)]
        if periodic:
            forward.append((count - 1, 0))
        backward = [(target, source) for source, target in forward]
        low = lax.ppermute(
            lax.slice_in_dim(block, block.shape[dim] - width, None, axis=dim), axis, forward
        )
        high = lax.ppermute(lax.slice_in_dim(block, 0, width, axis=dim), axis, backward)
        block = jnp.concatenate([low, block, high], axis=dim)
    return block


def valid_conv(padded, kernel):
    width_lon = padded.shape[1] - 2
    width_lat = padded.shape[2] - 2
    stacked = jnp.stack(
        [
            padded[:, row_shift : row_shift + width_lon, col_shift : col_shift + width_lat]
            for row_shift in range(3)
            for col_shift in range(3)
        ],
        0,
    )
    return jnp.einsum("toi,tixy->oxy", kernel, stacked, precision=lax.Precision.HIGHEST)


def embed_patches(field_in, patch_embed):
    chans, width_lon, width_lat = field_in.shape
    blocks = field_in.reshape(chans, width_lon // 2, 2, width_lat // 2, 2)
    embed_four = patch_embed.reshape(chans, 2, 2, patch_embed.shape[1])
    return jnp.einsum(
        "cpaqb,cabo->pqo", blocks, embed_four, preferred_element_type=jnp.float32
    ).astype(jnp.bfloat16)


def gelu_exact(v):
    return 0.5 * v * (1.0 + lax.erf(v * 0.7071067811865476))


def split_dot(rows, weights):
    high = rows.astype(jnp.bfloat16)
    low = (rows - high.astype(jnp.float32)).astype(jnp.bfloat16)
    w_high = weights.astype(jnp.bfloat16)
    w_low = (weights - w_high.astype(jnp.float32)).astype(jnp.bfloat16)
    dims = (((1,), (1,)), ((), ()))
    return (
        lax.dot_general(high, w_high, dims, preferred_element_type=jnp.float32)
        + lax.dot_general(low, w_high, dims, preferred_element_type=jnp.float32)
        + lax.dot_general(high, w_low, dims, preferred_element_type=jnp.float32)
    )


def row_conv(source, kt, product, lons, width, chans):
    count = (lons + 2) * width
    shifted = [source[pl.ds(s, count), :] for s in range(3)]
    product[pl.ds(0, count), :] = split_dot(jnp.concatenate(shifted, axis=1), kt)
    return sum(
        product[pl.ds(r * width, lons * width), r * chans : (r + 1) * chans] for r in range(3)
    )


def taps(kernel_ref):
    return jnp.concatenate(
        [jnp.concatenate([kernel_ref[3 * r + s] for s in range(3)], axis=1) for r in range(3)],
        axis=0,
    )


def lift_kernel(
    n, x_ref, k1_ref, k2_ref, pe_ref, w_ref, out_ref,
    xp, hp, fp, product, pes, pet, send_lo, send_hi, lat_lo, lat_hi, lon_lo, lon_hi, mine,
    tg, tt, wv, part, s_r, s_l, r_r, r_l,
    h_s, h_r, w_sem, ga_s, ga_r, gb_s, gb_r, gf_s, gf_r, rs_s, rs_r, ls_s, ls_r,
):
    z, x, s = lax.axis_index("tok"), lax.axis_index("ch"), lax.axis_index("sub")
    chunks, _, ob, hc = s_r.shape
    pieces = ga_s.shape[0]
    lons, lats, chans = x_ref.shape
    width = lats + 8
    dev = x * 2 + s
    last = 3

    def w_copy(c):
        return pltpu.make_async_copy(
            w_ref.at[:, pl.ds(pl.multiple_of(c * hc, hc), hc)], wv.at[c], w_sem.at[c]
        )

    barrier = pltpu.get_barrier_semaphore()
    up, down = lax.rem(z + 1, n), lax.rem(z + n - 1, n)
    for plane in (down, z, up):
        for dx in range(2):
            for ds in range(2):
                if plane is z and dx == 0 and ds == 0:
                    continue
                pl.semaphore_signal(
                    barrier, inc=1,
                    device_id={"tok": plane, "ch": lax.rem(x + dx, 2), "sub": lax.rem(s + ds, 2)},
                    device_id_type=MESH)

    for c in range(chunks):
        w_copy(c).start()
    send_lo[...] = x_ref[:, 0:2, :]
    send_hi[...] = x_ref[:, lats - 2 : lats, :]
    pl.semaphore_wait(barrier, 11)

    def halo(k, src, dst, plane, where):
        return pltpu.make_async_remote_copy(
            src, dst, h_s.at[k], h_r.at[k],
            device_id={"tok": plane, "ch": where // 2, "sub": lax.rem(where, 2)},
            device_id_type=MESH)

    low2, mid, high2 = pl.ds(0, 2), pl.ds(2, lons), pl.ds(lons + 2, 2)
    first2, last2 = pl.ds(0, 2), pl.ds(lons - 2, 2)
    lon_halos = (
        halo(0, x_ref.at[last2], lon_lo, up, dev),
        halo(1, x_ref.at[first2], lon_hi, down, dev),
    )

    def to_next():
        return (
            halo(2, send_hi.at[last2], lat_lo.at[low2], up, dev + 1),
            halo(3, send_hi.at[first2], lat_lo.at[high2], down, dev + 1),
            halo(4, send_hi, lat_lo.at[mid], z, dev + 1),
        )

    def to_before():
        return (
            halo(5, send_lo.at[last2], lat_hi.at[low2], up, dev - 1),
            halo(6, send_lo.at[first2], lat_hi.at[high2], down, dev - 1),
            halo(7, send_lo, lat_hi.at[mid], z, dev - 1),
        )

    for copy in lon_halos:
        copy.start()

    @pl.when(dev < last)
    def _():
        for copy in to_next():
            copy.start()

    @pl.when(dev > 0)
    def _():
        for copy in to_before():
            copy.start()

    xp[pl.ds(2, lons), pl.ds(2, lats), :] = x_ref[...]
    kt1 = taps(k1_ref)
    kt2 = taps(k2_ref)
    for t in range(pes.shape[0]):
        columns = pl.ds(t * 128, 128)
        pes[t] = pe_ref[:, columns].astype(jnp.float32)
        pet[columns, :] = jnp.transpose(
            jnp.concatenate([pes[t, pl.ds(j, chans, stride=4), :] for j in (0, 2, 1, 3)], axis=0)
        ).astype(jnp.bfloat16)

    @pl.when(dev == 0)
    def _():
        lat_lo[...] = jnp.zeros_like(lat_lo)

    @pl.when(dev == last)
    def _():
        lat_hi[...] = jnp.zeros_like(lat_hi)

    @pl.when(dev > 0)
    def _():
        for copy in to_next():
            copy.wait_recv()

    @pl.when(dev < last)
    def _():
        for copy in to_before():
            copy.wait_recv()

    for copy in lon_halos:
        copy.wait_recv()

    xp[pl.ds(0, 2), pl.ds(2, lats), :] = lon_lo[...]
    xp[pl.ds(lons + 2, 2), pl.ds(2, lats), :] = lon_hi[...]
    xp[pl.ds(0, lons + 4), pl.ds(0, 2), :] = lat_lo[...]
    xp[pl.ds(0, lons + 4), pl.ds(lats + 2, 2), :] = lat_hi[...]

    flat_x = xp.reshape((lons + 5) * width, chans)
    hidden = gelu_exact(row_conv(flat_x, kt1, product, lons + 2, width, chans))
    lat = lax.broadcasted_iota(jnp.int32, (lons + 2, width, chans), 1) + (dev * lats - 1)
    hidden = hidden.reshape(lons + 2, width, chans)
    hidden = jnp.where((lat >= 0) & (lat < 4 * lats), hidden, 0.0)
    hp[pl.ds(0, (lons + 2) * width), :] = hidden.reshape((lons + 2) * width, chans)
    field = row_conv(hp, kt2, product, lons, width, chans)
    field = field.astype(jnp.bfloat16).astype(jnp.float32)
    field = field.reshape(lons // 2, 2, width, chans)
    fp[...] = jnp.concatenate([field[:, 0], field[:, 1]], axis=2)
    mine[...] = jnp.concatenate(
        [fp[:, pl.ds(b, lats // 2, stride=2), :] for b in range(2)], axis=2
    ).astype(jnp.bfloat16)

    step = mine.shape[0] // pieces
    cross = (1 - x) * 2 + s
    copies = []
    for g in range(pieces):
        part_rows = pl.ds(g * step, step)
        copies.append((
            pltpu.make_async_remote_copy(
                mine.at[part_rows], tg.at[part_rows, dev], gb_s.at[g], gb_r.at[g],
                device_id={"ch": 1 - x}, device_id_type=MESH),
            pltpu.make_async_remote_copy(
                mine.at[part_rows], tg.at[part_rows, dev], ga_s.at[g], ga_r.at[g],
                device_id={"sub": 1 - s}, device_id_type=MESH),
            pltpu.make_async_remote_copy(
                tg.at[part_rows, cross], tg.at[part_rows, cross], gf_s.at[g], gf_r.at[g],
                device_id={"sub": 1 - s}, device_id_type=MESH),
        ))
    for over_x, over_s, _ in copies:
        over_x.start()
        over_s.start()
    tg[:, dev] = mine[...]
    for over_x, _, onward in copies:
        over_x.wait_recv()
        onward.start()
    for over_x, over_s, onward in copies:
        over_s.wait_recv()
        onward.wait_recv()
        over_x.wait_send()
        over_s.wait_send()
        onward.wait_send()
    for copy in lon_halos:
        copy.wait_send()

    @pl.when(dev < last)
    def _():
        for copy in to_next():
            copy.wait_send()

    @pl.when(dev > 0)
    def _():
        for copy in to_before():
            copy.wait_send()

    flat = tg[...].reshape(tt.shape[1], pet.shape[1])
    tt[...] = lax.dot_general(
        pet[...], flat, (((1,), (1,)), ((), ())), preferred_element_type=jnp.float32
    ).astype(jnp.bfloat16)

    def right_copy(c, d):
        return pltpu.make_async_remote_copy(
            s_r.at[c, d], r_r.at[c, d], rs_s.at[c, d], rs_r.at[c, d],
            device_id={"tok": z + 1}, device_id_type=MESH)

    def left_copy(c, d):
        return pltpu.make_async_remote_copy(
            s_l.at[c, d], r_l.at[c, d], ls_s.at[c, d], ls_r.at[c, d],
            device_id={"tok": z - 1}, device_id_type=MESH)

    def compute(c, carry):
        w_copy(c).wait()
        product = jnp.dot(tt[...], wv[c], preferred_element_type=jnp.float32)
        part[c] = product.reshape(n, ob, hc)

        @pl.when(z == 0)
        def _():
            for d in range(n - 1, 0, -1):
                s_r[c, d] = part[c, d].astype(jnp.bfloat16)
                right_copy(c, d).start()

        @pl.when(z == n - 1)
        def _():
            for d in range(n - 1):
                s_l[c, d] = part[c, d].astype(jnp.bfloat16)
                left_copy(c, d).start()

        return carry

    lax.fori_loop(0, chunks, compute, 0)

    right_lag = jnp.maximum(z - 1, 0) * LAG
    left_lag = jnp.maximum(n - 2 - z, 0) * LAG
    last_lag = jnp.maximum(right_lag, left_lag)

    def forward(i, carry):
        c_r, c_l, c_o = i - right_lag, i - left_lag, i - last_lag
        for d in range(n - 1, 0, -1):
            @pl.when((z > 0) & (z < d) & (c_r >= 0) & (c_r < chunks))
            def _():
                right_copy(c_r, d).wait_recv()
                s_r[c_r, d] = (part[c_r, d] + r_r[c_r, d].astype(jnp.float32)).astype(jnp.bfloat16)
                right_copy(c_r, d).start()

        for d in range(n - 1):
            @pl.when((z < n - 1) & (z > d) & (c_l >= 0) & (c_l < chunks))
            def _():
                left_copy(c_l, d).wait_recv()
                s_l[c_l, d] = (part[c_l, d] + r_l[c_l, d].astype(jnp.float32)).astype(jnp.bfloat16)
                left_copy(c_l, d).start()

        for d in range(n):
            @pl.when((z == d) & (c_o >= 0) & (c_o < chunks))
            def _():
                total = part[c_o, d]
                if d > 0:
                    right_copy(c_o, d).wait_recv()
                    total = total + r_r[c_o, d].astype(jnp.float32)
                if d < n - 1:
                    left_copy(c_o, d).wait_recv()
                    total = total + r_l[c_o, d].astype(jnp.float32)
                out_ref[:, pl.ds(pl.multiple_of(c_o * hc, hc), hc)] = gelu_exact(total).astype(out_ref.dtype)

        return carry

    lax.fori_loop(0, chunks + (n - 2) * LAG, forward, 0)

    def drain(c, carry):
        for d in range(n):
            @pl.when(z < d)
            def _():
                right_copy(c, d).wait_send()

            @pl.when(z > d)
            def _():
                left_copy(c, d).wait_send()

        return carry

    lax.fori_loop(0, chunks, drain, 0)


def lift(turned, conv_first, conv_second, patch_embed, token_mixing):
    n = lax.axis_size("tok")
    lons, lats, chans = turned.shape
    embed = patch_embed.shape[1]
    depth, cols = token_mixing.shape
    hc = cols // CHUNKS
    ob = embed // n
    width = lats + 8
    dma, bf16, f32 = pltpu.SemaphoreType.DMA, jnp.bfloat16, jnp.float32
    blocks = pltpu.VMEM((CHUNKS, n, ob, hc), bf16)
    held = pl.BlockSpec(memory_space=pltpu.VMEM)
    return pl.pallas_call(
        functools.partial(lift_kernel, n),
        out_shape=jax.ShapeDtypeStruct((ob, cols), bf16),
        in_specs=[held, held, held, held, pl.BlockSpec(memory_space=pl.ANY)],
        out_specs=held,
        scratch_shapes=[
            pltpu.VMEM((lons + 5, width, chans), f32),
            pltpu.VMEM(((lons + 3) * width, chans), f32),
            pltpu.VMEM((lons // 2, width, 2 * chans), f32),
            pltpu.VMEM(((lons + 4) * width, 3 * chans), f32),
            pltpu.VMEM((embed // 128, 4 * chans, 128), f32),
            pltpu.VMEM((embed, 4 * chans), bf16),
            pltpu.VMEM((lons, 2, chans), f32),
            pltpu.VMEM((lons, 2, chans), f32),
            pltpu.VMEM((lons + 4, 2, chans), f32),
            pltpu.VMEM((lons + 4, 2, chans), f32),
            pltpu.VMEM((2, lats, chans), f32),
            pltpu.VMEM((2, lats, chans), f32),
            pltpu.VMEM((lons // 2, lats // 2, 4 * chans), bf16),
            pltpu.VMEM((lons // 2, 4, lats // 2, 4 * chans), bf16),
            pltpu.VMEM((embed, depth), bf16),
            pltpu.VMEM((CHUNKS, depth, hc), bf16),
            pltpu.VMEM((CHUNKS, n, ob, hc), f32),
            blocks, blocks, blocks, blocks,
            dma((8,)), dma((8,)), dma((CHUNKS,)),
        ] + [dma((PIECES,))] * 6 + [dma((CHUNKS, n))] * 4,
        compiler_params=pltpu.CompilerParams(
            collective_id=0, has_side_effects=True, vmem_limit_bytes=60 * 1024 * 1024
        ),
    )(turned, conv_first, conv_second, patch_embed, token_mixing)


def fits(weather, token_mixing, embed):
    n = lax.axis_size("tok")
    return (
        lax.axis_size("ch") == 2
        and lax.axis_size("sub") == 2
        and 2 < n <= 8
        and embed % (16 * n) == 0
        and token_mixing.shape[1] % (128 * CHUNKS) == 0
        and weather.shape[1] % (4 * PIECES) == 0
        and weather.shape[2] % 32 == 0
        and 2 * weather.shape[0] == 128
        and embed % 128 == 0
    )


def local(weather, conv_first, conv_second, patch_embed, token_mixing):
    if fits(weather, token_mixing, patch_embed.shape[1]):
        turned = jnp.transpose(weather, (1, 2, 0))
        return lift(turned, conv_first, conv_second, patch_embed, token_mixing)
    widened = padded_2(weather, (("tok", 1),), 2, True)
    padded = padded_2(widened, ((("ch", "sub"), 2),), 2, False)
    hidden_one = jax.nn.gelu(valid_conv(padded, conv_first), approximate=False)
    width_lat = weather.shape[2]
    lat_index = (
        jnp.arange(width_lat + 2, dtype=jnp.int32) - 1 + lax.axis_index(("ch", "sub")) * width_lat
    )
    inside = (lat_index >= 0) & (lat_index < width_lat * lax.axis_size(("ch", "sub")))
    hidden_one = jnp.where(inside[None, None, :], hidden_one, jnp.float32(0.0))
    field_two = valid_conv(hidden_one, conv_second)
    field_two = field_two.astype(jnp.bfloat16)
    local_tokens = embed_patches(field_two, patch_embed)
    gathered = lax.all_gather(local_tokens, ("ch", "sub"), axis=1, tiled=True)
    tokens = gathered.reshape(-1, gathered.shape[2])
    summed = lax.psum_scatter(
        lax.dot_general(
            tokens, token_mixing, (((0,), (0,)), ((), ())), preferred_element_type=jnp.float32
        ),
        "tok",
        scatter_dimension=0,
        tiled=True,
    )
    return jax.nn.gelu(summed, approximate=False).astype(jnp.bfloat16)


def solution(mesh):
    placed = (P("groups", "tok", ("ch", "sub")), P(), P(), P(), P("tok", ("ch", "sub")))
    return jax.shard_map(
        local,
        mesh=mesh,
        in_specs=placed,
        out_specs=P(("groups", "tok"), ("ch", "sub")),
        check_vma=False,
    )
```

```python
import functools

import jax
import jax.numpy as jnp
from jax import lax
from jax.experimental import pallas as pl
from jax.experimental.pallas import tpu as pltpu
from jax.sharding import PartitionSpec as P

MESH = pl.DeviceIdType.MESH
CHUNKS = 4
PIECES = 2
LAG = 1
DELAY = 1


def padded_2(block, sides, width, periodic):
    for axis, dim in sides:
        count = lax.axis_size(axis)
        forward = [(i, i + 1) for i in range(count - 1)]
        if periodic:
            forward.append((count - 1, 0))
        backward = [(target, source) for source, target in forward]
        low = lax.ppermute(
            lax.slice_in_dim(block, block.shape[dim] - width, None, axis=dim), axis, forward
        )
        high = lax.ppermute(lax.slice_in_dim(block, 0, width, axis=dim), axis, backward)
        block = jnp.concatenate([low, block, high], axis=dim)
    return block


def valid_conv(padded, kernel):
    width_lon = padded.shape[1] - 2
    width_lat = padded.shape[2] - 2
    stacked = jnp.stack(
        [
            padded[:, row_shift : row_shift + width_lon, col_shift : col_shift + width_lat]
            for row_shift in range(3)
            for col_shift in range(3)
        ],
        0,
    )
    return jnp.einsum("toi,tixy->oxy", kernel, stacked, precision=lax.Precision.HIGHEST)


def embed_patches(field_in, patch_embed):
    chans, width_lon, width_lat = field_in.shape
    blocks = field_in.reshape(chans, width_lon // 2, 2, width_lat // 2, 2)
    embed_four = patch_embed.reshape(chans, 2, 2, patch_embed.shape[1])
    return jnp.einsum(
        "cpaqb,cabo->pqo", blocks, embed_four, preferred_element_type=jnp.float32
    ).astype(jnp.bfloat16)


def gelu_exact(v):
    return 0.5 * v * (1.0 + lax.erf(v * 0.7071067811865476))


def split_dot(rows, weights):
    high = rows.astype(jnp.bfloat16)
    low = (rows - high.astype(jnp.float32)).astype(jnp.bfloat16)
    w_high = weights.astype(jnp.bfloat16)
    w_low = (weights - w_high.astype(jnp.float32)).astype(jnp.bfloat16)
    dims = (((1,), (1,)), ((), ()))
    return (
        lax.dot_general(high, w_high, dims, preferred_element_type=jnp.float32)
        + lax.dot_general(low, w_high, dims, preferred_element_type=jnp.float32)
        + lax.dot_general(high, w_low, dims, preferred_element_type=jnp.float32)
    )


def row_conv(source, kt, product, first, lons, width, chans):
    count = (lons + 2) * width
    shifted = [source[pl.ds(first * width + s, count), :] for s in range(3)]
    product[pl.ds(0, count), :] = split_dot(jnp.concatenate(shifted, axis=1), kt)
    return sum(
        product[pl.ds(r * width, lons * width), r * chans : (r + 1) * chans] for r in range(3)
    )


def taps(kernel_ref):
    return jnp.concatenate(
        [jnp.concatenate([kernel_ref[3 * r + s] for s in range(3)], axis=1) for r in range(3)],
        axis=0,
    )


def lift_kernel(
    n, x_in, k1_in, k2_in, pe_in, w_ref, out_ref,
    x_ref, k1_ref, k2_ref, pe_ref,
    xp, hp, fp, product, pes, pet, send_lo, send_hi, lat_lo, lat_hi, lon_lo, lon_hi, mine,
    tg, tt, wv, part, s_r, s_l, r_r, r_l,
    in_sem, h_s, h_r, w_sem, ga_s, ga_r, gb_s, gb_r, gf_s, gf_r, rs_s, rs_r, ls_s, ls_r,
):
    z, x, s = lax.axis_index("tok"), lax.axis_index("ch"), lax.axis_index("sub")
    chunks, _, ob, hc = s_r.shape
    pieces = ga_s.shape[0]
    lons, lats, chans = x_in.shape
    width = lats + 8
    dev = x * 2 + s
    last = 3

    def w_copy(c):
        return pltpu.make_async_copy(
            w_ref.at[:, pl.ds(pl.multiple_of(c * hc, hc), hc)], wv.at[c], w_sem.at[c]
        )

    fetches = [
        pltpu.make_async_copy(src, dst, in_sem.at[k])
        for k, (src, dst) in enumerate(
            ((x_in, x_ref), (k1_in, k1_ref), (k2_in, k2_ref), (pe_in, pe_ref))
        )
    ]
    fetches[0].start()
    barrier = pltpu.get_barrier_semaphore()
    up, down = lax.rem(z + 1, n), lax.rem(z + n - 1, n)
    for plane in (down, z, up):
        for dx in range(2):
            for ds in range(2):
                if plane is z and dx == 0 and ds == 0:
                    continue
                pl.semaphore_signal(
                    barrier, inc=1,
                    device_id={"tok": plane, "ch": lax.rem(x + dx, 2), "sub": lax.rem(s + ds, 2)},
                    device_id_type=MESH)

    for copy in fetches[1:]:
        copy.start()
    for c in range(chunks):
        w_copy(c).start()
    fetches[0].wait()
    send_lo[...] = x_ref[:, 0:2, :]
    send_hi[...] = x_ref[:, lats - 2 : lats, :]
    pl.semaphore_wait(barrier, 11)

    def halo(k, src, dst, plane, where):
        return pltpu.make_async_remote_copy(
            src, dst, h_s.at[k], h_r.at[k],
            device_id={"tok": plane, "ch": where // 2, "sub": lax.rem(where, 2)},
            device_id_type=MESH)

    low2, mid, high2 = pl.ds(0, 2), pl.ds(2, lons), pl.ds(lons + 2, 2)
    first2, last2 = pl.ds(0, 2), pl.ds(lons - 2, 2)
    lon_halos = (
        halo(0, x_ref.at[last2], lon_lo, up, dev),
        halo(1, x_ref.at[first2], lon_hi, down, dev),
    )

    def to_next():
        return (
            halo(2, send_hi.at[last2], lat_lo.at[low2], up, dev + 1),
            halo(3, send_hi.at[first2], lat_lo.at[high2], down, dev + 1),
            halo(4, send_hi, lat_lo.at[mid], z, dev + 1),
        )

    def to_before():
        return (
            halo(5, send_lo.at[last2], lat_hi.at[low2], up, dev - 1),
            halo(6, send_lo.at[first2], lat_hi.at[high2], down, dev - 1),
            halo(7, send_lo, lat_hi.at[mid], z, dev - 1),
        )

    for copy in lon_halos:
        copy.start()

    @pl.when(dev < last)
    def _():
        for copy in to_next():
            copy.start()

    @pl.when(dev > 0)
    def _():
        for copy in to_before():
            copy.start()

    xp[pl.ds(2, lons), pl.ds(2, lats), :] = x_ref[...]
    for copy in fetches[1:]:
        copy.wait()
    kt1 = taps(k1_ref)
    kt2 = taps(k2_ref)
    for t in range(pes.shape[0]):
        columns = pl.ds(t * 128, 128)
        pes[t] = pe_ref[:, columns].astype(jnp.float32)
        pet[columns, :] = jnp.transpose(
            jnp.concatenate([pes[t, pl.ds(j, chans, stride=4), :] for j in (0, 2, 1, 3)], axis=0)
        ).astype(jnp.bfloat16)

    @pl.when(dev == 0)
    def _():
        lat_lo[...] = jnp.zeros_like(lat_lo)

    @pl.when(dev == last)
    def _():
        lat_hi[...] = jnp.zeros_like(lat_hi)

    @pl.when(dev > 0)
    def _():
        to_next()[2].wait_recv()

    @pl.when(dev < last)
    def _():
        to_before()[2].wait_recv()

    xp[mid, pl.ds(0, 2), :] = lat_lo[mid]
    xp[mid, pl.ds(lats + 2, 2), :] = lat_hi[mid]
    flat_x = xp.reshape((lons + 5) * width, chans)

    def hide(first, count):
        hidden = gelu_exact(row_conv(flat_x, kt1, product, first, count, width, chans))
        lat = lax.broadcasted_iota(jnp.int32, (count, width, chans), 1) + (dev * lats - 1)
        hidden = hidden.reshape(count, width, chans)
        hidden = jnp.where((lat >= 0) & (lat < 4 * lats), hidden, 0.0)
        hp[pl.ds(first * width, count * width), :] = hidden.reshape(count * width, chans)

    hide(2, lons - 2)

    @pl.when(dev > 0)
    def _():
        for copy in to_next()[:2]:
            copy.wait_recv()

    @pl.when(dev < last)
    def _():
        for copy in to_before()[:2]:
            copy.wait_recv()

    for copy in lon_halos:
        copy.wait_recv()

    xp[low2, pl.ds(2, lats), :] = lon_lo[...]
    xp[high2, pl.ds(2, lats), :] = lon_hi[...]
    for side in (low2, high2):
        xp[side, pl.ds(0, 2), :] = lat_lo[side]
        xp[side, pl.ds(lats + 2, 2), :] = lat_hi[side]
    hide(0, 2)
    hide(lons, 2)

    step = mine.shape[0] // pieces
    cross = (1 - x) * 2 + s
    copies = []
    for g in range(pieces):
        part_rows = pl.ds(g * step, step)
        copies.append((
            pltpu.make_async_remote_copy(
                mine.at[part_rows], tg.at[part_rows, dev], gb_s.at[g], gb_r.at[g],
                device_id={"ch": 1 - x}, device_id_type=MESH),
            pltpu.make_async_remote_copy(
                mine.at[part_rows], tg.at[part_rows, dev], ga_s.at[g], ga_r.at[g],
                device_id={"sub": 1 - s}, device_id_type=MESH),
            pltpu.make_async_remote_copy(
                tg.at[part_rows, cross], tg.at[part_rows, cross], gf_s.at[g], gf_r.at[g],
                device_id={"sub": 1 - s}, device_id_type=MESH),
        ))
    for g, (over_x, over_s, _) in enumerate(copies):
        count = 2 * step
        field = row_conv(hp, kt2, product, g * count, count, width, chans)
        field = field.astype(jnp.bfloat16).astype(jnp.float32)
        field = field.reshape(step, 2, width, chans)
        fp[...] = jnp.concatenate([field[:, 0], field[:, 1]], axis=2)
        mine[pl.ds(g * step, step)] = jnp.concatenate(
            [fp[:, pl.ds(b, lats // 2, stride=2), :] for b in range(2)], axis=2
        ).astype(jnp.bfloat16)
        over_x.start()
        over_s.start()
    tg[:, dev] = mine[...]
    for over_x, _, onward in copies:
        over_x.wait_recv()
        onward.start()
    for over_x, over_s, onward in copies:
        over_s.wait_recv()
        onward.wait_recv()
        over_x.wait_send()
        over_s.wait_send()
        onward.wait_send()
    for copy in lon_halos:
        copy.wait_send()

    @pl.when(dev < last)
    def _():
        for copy in to_next():
            copy.wait_send()

    @pl.when(dev > 0)
    def _():
        for copy in to_before():
            copy.wait_send()

    flat = tg[...].reshape(tt.shape[1], pet.shape[1])
    tt[...] = lax.dot_general(
        pet[...], flat, (((1,), (1,)), ((), ())), preferred_element_type=jnp.float32
    ).astype(jnp.bfloat16)

    def right_copy(c, d):
        return pltpu.make_async_remote_copy(
            s_r.at[c, d], r_r.at[c, d], rs_s.at[c, d], rs_r.at[c, d],
            device_id={"tok": z + 1}, device_id_type=MESH)

    def left_copy(c, d):
        return pltpu.make_async_remote_copy(
            s_l.at[c, d], r_l.at[c, d], ls_s.at[c, d], ls_r.at[c, d],
            device_id={"tok": z - 1}, device_id_type=MESH)

    def sources(i):
        for d in range(n - 1, 0, -1):
            c = i - (n - 1 - d) * DELAY

            @pl.when((z == 0) & (c >= 0) & (c < chunks))
            def _():
                s_r[c, d] = part[c, d].astype(jnp.bfloat16)
                right_copy(c, d).start()

        for d in range(n - 1):
            c = i - d * DELAY

            @pl.when((z == n - 1) & (c >= 0) & (c < chunks))
            def _():
                s_l[c, d] = part[c, d].astype(jnp.bfloat16)
                left_copy(c, d).start()

    def compute(c, carry):
        w_copy(c).wait()
        product = jnp.dot(tt[...], wv[c], preferred_element_type=jnp.float32)
        part[c] = product.reshape(n, ob, hc)

        sources(c)
        return carry

    lax.fori_loop(0, chunks, compute, 0)
    for late in range((n - 2) * DELAY):
        sources(chunks + late)

    right_lag = jnp.maximum(z - 1, 0) * LAG
    left_lag = jnp.maximum(n - 2 - z, 0) * LAG
    last_lag = jnp.maximum(right_lag + (n - 1 - z) * DELAY, left_lag + z * DELAY)

    def forward(i, carry):
        c_o = i - last_lag
        for d in range(n - 1, 0, -1):
            c_r = i - right_lag - (n - 1 - d) * DELAY

            @pl.when((z > 0) & (z < d) & (c_r >= 0) & (c_r < chunks))
            def _():
                right_copy(c_r, d).wait_recv()
                s_r[c_r, d] = (part[c_r, d] + r_r[c_r, d].astype(jnp.float32)).astype(jnp.bfloat16)
                right_copy(c_r, d).start()

        for d in range(n - 1):
            c_l = i - left_lag - d * DELAY

            @pl.when((z < n - 1) & (z > d) & (c_l >= 0) & (c_l < chunks))
            def _():
                left_copy(c_l, d).wait_recv()
                s_l[c_l, d] = (part[c_l, d] + r_l[c_l, d].astype(jnp.float32)).astype(jnp.bfloat16)
                left_copy(c_l, d).start()

        for d in range(n):
            @pl.when((z == d) & (c_o >= 0) & (c_o < chunks))
            def _():
                total = part[c_o, d]
                if d > 0:
                    right_copy(c_o, d).wait_recv()
                    total = total + r_r[c_o, d].astype(jnp.float32)
                if d < n - 1:
                    left_copy(c_o, d).wait_recv()
                    total = total + r_l[c_o, d].astype(jnp.float32)
                out_ref[:, pl.ds(pl.multiple_of(c_o * hc, hc), hc)] = gelu_exact(total).astype(out_ref.dtype)

        return carry

    lax.fori_loop(0, chunks + (n - 1) * DELAY + (n - 2) * LAG, forward, 0)

    def drain(c, carry):
        for d in range(n):
            @pl.when(z < d)
            def _():
                right_copy(c, d).wait_send()

            @pl.when(z > d)
            def _():
                left_copy(c, d).wait_send()

        return carry

    lax.fori_loop(0, chunks, drain, 0)


def lift(turned, conv_first, conv_second, patch_embed, token_mixing):
    n = lax.axis_size("tok")
    lons, lats, chans = turned.shape
    embed = patch_embed.shape[1]
    depth, cols = token_mixing.shape
    hc = cols // CHUNKS
    ob = embed // n
    width = lats + 8
    dma, bf16, f32 = pltpu.SemaphoreType.DMA, jnp.bfloat16, jnp.float32
    blocks = pltpu.VMEM((CHUNKS, n, ob, hc), bf16)
    held = pl.BlockSpec(memory_space=pltpu.VMEM)
    return pl.pallas_call(
        functools.partial(lift_kernel, n),
        out_shape=jax.ShapeDtypeStruct((ob, cols), bf16),
        in_specs=[pl.BlockSpec(memory_space=pl.ANY)] * 5,
        out_specs=held,
        scratch_shapes=[
            pltpu.VMEM(turned.shape, f32),
            pltpu.VMEM(conv_first.shape, f32),
            pltpu.VMEM(conv_second.shape, f32),
            pltpu.VMEM(patch_embed.shape, bf16),
            pltpu.VMEM((lons + 5, width, chans), f32),
            pltpu.VMEM(((lons + 3) * width, chans), f32),
            pltpu.VMEM((lons // 2 // PIECES, width, 2 * chans), f32),
            pltpu.VMEM(((lons + 4) * width, 3 * chans), f32),
            pltpu.VMEM((embed // 128, 4 * chans, 128), f32),
            pltpu.VMEM((embed, 4 * chans), bf16),
            pltpu.VMEM((lons, 2, chans), f32),
            pltpu.VMEM((lons, 2, chans), f32),
            pltpu.VMEM((lons + 4, 2, chans), f32),
            pltpu.VMEM((lons + 4, 2, chans), f32),
            pltpu.VMEM((2, lats, chans), f32),
            pltpu.VMEM((2, lats, chans), f32),
            pltpu.VMEM((lons // 2, lats // 2, 4 * chans), bf16),
            pltpu.VMEM((lons // 2, 4, lats // 2, 4 * chans), bf16),
            pltpu.VMEM((embed, depth), bf16),
            pltpu.VMEM((CHUNKS, depth, hc), bf16),
            pltpu.VMEM((CHUNKS, n, ob, hc), f32),
            blocks, blocks, blocks, blocks,
            dma((4,)), dma((8,)), dma((8,)), dma((CHUNKS,)),
        ] + [dma((PIECES,))] * 6 + [dma((CHUNKS, n))] * 4,
        compiler_params=pltpu.CompilerParams(
            collective_id=0, has_side_effects=True, vmem_limit_bytes=60 * 1024 * 1024
        ),
    )(turned, conv_first, conv_second, patch_embed, token_mixing)


def fits(weather, token_mixing, embed):
    n = lax.axis_size("tok")
    return (
        lax.axis_size("ch") == 2
        and lax.axis_size("sub") == 2
        and 2 < n <= 8
        and embed % (16 * n) == 0
        and token_mixing.shape[1] % (128 * CHUNKS) == 0
        and weather.shape[1] % (4 * PIECES) == 0
        and weather.shape[2] % 32 == 0
        and 2 * weather.shape[0] == 128
        and embed % 128 == 0
    )


def local(weather, conv_first, conv_second, patch_embed, token_mixing):
    if fits(weather, token_mixing, patch_embed.shape[1]):
        turned = jnp.transpose(weather, (1, 2, 0))
        return lift(turned, conv_first, conv_second, patch_embed, token_mixing)
    widened = padded_2(weather, (("tok", 1),), 2, True)
    padded = padded_2(widened, ((("ch", "sub"), 2),), 2, False)
    hidden_one = jax.nn.gelu(valid_conv(padded, conv_first), approximate=False)
    width_lat = weather.shape[2]
    lat_index = (
        jnp.arange(width_lat + 2, dtype=jnp.int32) - 1 + lax.axis_index(("ch", "sub")) * width_lat
    )
    inside = (lat_index >= 0) & (lat_index < width_lat * lax.axis_size(("ch", "sub")))
    hidden_one = jnp.where(inside[None, None, :], hidden_one, jnp.float32(0.0))
    field_two = valid_conv(hidden_one, conv_second)
    field_two = field_two.astype(jnp.bfloat16)
    local_tokens = embed_patches(field_two, patch_embed)
    gathered = lax.all_gather(local_tokens, ("ch", "sub"), axis=1, tiled=True)
    tokens = gathered.reshape(-1, gathered.shape[2])
    summed = lax.psum_scatter(
        lax.dot_general(
            tokens, token_mixing, (((0,), (0,)), ((), ())), preferred_element_type=jnp.float32
        ),
        "tok",
        scatter_dimension=0,
        tiled=True,
    )
    return jax.nn.gelu(summed, approximate=False).astype(jnp.bfloat16)


def solution(mesh):
    placed = (P("groups", "tok", ("ch", "sub")), P(), P(), P(), P("tok", ("ch", "sub")))
    return jax.shard_map(
        local,
        mesh=mesh,
        in_specs=placed,
        out_specs=P(("groups", "tok"), ("ch", "sub")),
        check_vma=False,
    )
```

```python
import functools

import jax
import jax.numpy as jnp
from jax import lax
from jax.experimental import pallas as pl
from jax.experimental.pallas import tpu as pltpu
from jax.sharding import PartitionSpec as P

MESH = pl.DeviceIdType.MESH
CHUNKS = 4
PIECES = 2
LAG = 1
DELAY = 1


def padded_2(block, sides, width, periodic):
    for axis, dim in sides:
        count = lax.axis_size(axis)
        forward = [(i, i + 1) for i in range(count - 1)]
        if periodic:
            forward.append((count - 1, 0))
        backward = [(target, source) for source, target in forward]
        low = lax.ppermute(
            lax.slice_in_dim(block, block.shape[dim] - width, None, axis=dim), axis, forward
        )
        high = lax.ppermute(lax.slice_in_dim(block, 0, width, axis=dim), axis, backward)
        block = jnp.concatenate([low, block, high], axis=dim)
    return block


def valid_conv(padded, kernel):
    width_lon = padded.shape[1] - 2
    width_lat = padded.shape[2] - 2
    stacked = jnp.stack(
        [
            padded[:, row_shift : row_shift + width_lon, col_shift : col_shift + width_lat]
            for row_shift in range(3)
            for col_shift in range(3)
        ],
        0,
    )
    return jnp.einsum("toi,tixy->oxy", kernel, stacked, precision=lax.Precision.HIGHEST)


def embed_patches(field_in, patch_embed):
    chans, width_lon, width_lat = field_in.shape
    blocks = field_in.reshape(chans, width_lon // 2, 2, width_lat // 2, 2)
    embed_four = patch_embed.reshape(chans, 2, 2, patch_embed.shape[1])
    return jnp.einsum(
        "cpaqb,cabo->pqo", blocks, embed_four, preferred_element_type=jnp.float32
    ).astype(jnp.bfloat16)


def gelu_exact(v):
    return 0.5 * v * (1.0 + lax.erf(v * 0.7071067811865476))


def split_dot(rows, weights):
    high = rows.astype(jnp.bfloat16)
    low = (rows - high.astype(jnp.float32)).astype(jnp.bfloat16)
    w_high = weights.astype(jnp.bfloat16)
    w_low = (weights - w_high.astype(jnp.float32)).astype(jnp.bfloat16)
    dims = (((1,), (1,)), ((), ()))
    return (
        lax.dot_general(high, w_high, dims, preferred_element_type=jnp.float32)
        + lax.dot_general(low, w_high, dims, preferred_element_type=jnp.float32)
        + lax.dot_general(high, w_low, dims, preferred_element_type=jnp.float32)
    )


def row_conv(source, kt, product, first, lons, width, chans):
    count = (lons + 2) * width
    shifted = [source[pl.ds(first * width + s, count), :] for s in range(3)]
    product[pl.ds(0, count), :] = split_dot(jnp.concatenate(shifted, axis=1), kt)
    return sum(
        product[pl.ds(r * width, lons * width), r * chans : (r + 1) * chans] for r in range(3)
    )


def taps(kernel_ref):
    return jnp.concatenate(
        [jnp.concatenate([kernel_ref[3 * r + s] for s in range(3)], axis=1) for r in range(3)],
        axis=0,
    )


def lift_kernel(
    n, x_in, k1_in, k2_in, pe_in, w_ref, out_ref,
    x_ref, k1_ref, k2_ref, pe_ref,
    xp, hp, fp, product, pes, pet, send_lo, send_hi, lat_lo, lat_hi, lon_lo, lon_hi, mine,
    tg, tt, wv, done, part, s_r, s_l, r_r, r_l,
    in_sem, h_s, h_r, w_sem, o_sem, ga_s, ga_r, gb_s, gb_r, gf_s, gf_r, rs_s, rs_r, ls_s, ls_r,
):
    z, x, s = lax.axis_index("tok"), lax.axis_index("ch"), lax.axis_index("sub")
    chunks, _, ob, hc = s_r.shape
    pieces = ga_s.shape[0]
    lons, lats, chans = x_in.shape
    width = lats + 8
    dev = x * 2 + s
    last = 3

    def w_copy(c):
        return pltpu.make_async_copy(
            w_ref.at[:, pl.ds(pl.multiple_of(c * hc, hc), hc)], wv.at[c], w_sem.at[c]
        )

    fetches = [
        pltpu.make_async_copy(src, dst, in_sem.at[k])
        for k, (src, dst) in enumerate(
            ((x_in, x_ref), (k1_in, k1_ref), (k2_in, k2_ref), (pe_in, pe_ref))
        )
    ]
    fetches[0].start()
    barrier = pltpu.get_barrier_semaphore()
    up, down = lax.rem(z + 1, n), lax.rem(z + n - 1, n)
    for plane in (down, z, up):
        for dx in range(2):
            for ds in range(2):
                if plane is z and dx == 0 and ds == 0:
                    continue
                pl.semaphore_signal(
                    barrier, inc=1,
                    device_id={"tok": plane, "ch": lax.rem(x + dx, 2), "sub": lax.rem(s + ds, 2)},
                    device_id_type=MESH)

    for copy in fetches[1:]:
        copy.start()
    for c in range(chunks):
        w_copy(c).start()
    fetches[0].wait()
    send_lo[...] = x_ref[:, 0:2, :]
    send_hi[...] = x_ref[:, lats - 2 : lats, :]
    pl.semaphore_wait(barrier, 11)

    def halo(k, src, dst, plane, where):
        return pltpu.make_async_remote_copy(
            src, dst, h_s.at[k], h_r.at[k],
            device_id={"tok": plane, "ch": where // 2, "sub": lax.rem(where, 2)},
            device_id_type=MESH)

    low2, mid, high2 = pl.ds(0, 2), pl.ds(2, lons), pl.ds(lons + 2, 2)
    first2, last2 = pl.ds(0, 2), pl.ds(lons - 2, 2)
    lon_halos = (
        halo(0, x_ref.at[last2], lon_lo, up, dev),
        halo(1, x_ref.at[first2], lon_hi, down, dev),
    )

    def to_next():
        return (
            halo(2, send_hi.at[last2], lat_lo.at[low2], up, dev + 1),
            halo(3, send_hi.at[first2], lat_lo.at[high2], down, dev + 1),
            halo(4, send_hi, lat_lo.at[mid], z, dev + 1),
        )

    def to_before():
        return (
            halo(5, send_lo.at[last2], lat_hi.at[low2], up, dev - 1),
            halo(6, send_lo.at[first2], lat_hi.at[high2], down, dev - 1),
            halo(7, send_lo, lat_hi.at[mid], z, dev - 1),
        )

    for copy in lon_halos:
        copy.start()

    @pl.when(dev < last)
    def _():
        for copy in to_next():
            copy.start()

    @pl.when(dev > 0)
    def _():
        for copy in to_before():
            copy.start()

    xp[pl.ds(2, lons), pl.ds(2, lats), :] = x_ref[...]
    for copy in fetches[1:]:
        copy.wait()
    kt1 = taps(k1_ref)
    kt2 = taps(k2_ref)
    for t in range(pes.shape[0]):
        columns = pl.ds(t * 128, 128)
        pes[t] = pe_ref[:, columns].astype(jnp.float32)
        pet[columns, :] = jnp.transpose(
            jnp.concatenate([pes[t, pl.ds(j, chans, stride=4), :] for j in (0, 2, 1, 3)], axis=0)
        ).astype(jnp.bfloat16)

    @pl.when(dev == 0)
    def _():
        lat_lo[...] = jnp.zeros_like(lat_lo)

    @pl.when(dev == last)
    def _():
        lat_hi[...] = jnp.zeros_like(lat_hi)

    @pl.when(dev > 0)
    def _():
        to_next()[2].wait_recv()

    @pl.when(dev < last)
    def _():
        to_before()[2].wait_recv()

    xp[mid, pl.ds(0, 2), :] = lat_lo[mid]
    xp[mid, pl.ds(lats + 2, 2), :] = lat_hi[mid]
    flat_x = xp.reshape((lons + 5) * width, chans)

    def hide(first, count):
        hidden = gelu_exact(row_conv(flat_x, kt1, product, first, count, width, chans))
        lat = lax.broadcasted_iota(jnp.int32, (count, width, chans), 1) + (dev * lats - 1)
        hidden = hidden.reshape(count, width, chans)
        hidden = jnp.where((lat >= 0) & (lat < 4 * lats), hidden, 0.0)
        hp[pl.ds(first * width, count * width), :] = hidden.reshape(count * width, chans)

    hide(2, lons - 2)

    @pl.when(dev > 0)
    def _():
        for copy in to_next()[:2]:
            copy.wait_recv()

    @pl.when(dev < last)
    def _():
        for copy in to_before()[:2]:
            copy.wait_recv()

    for copy in lon_halos:
        copy.wait_recv()

    xp[low2, pl.ds(2, lats), :] = lon_lo[...]
    xp[high2, pl.ds(2, lats), :] = lon_hi[...]
    for side in (low2, high2):
        xp[side, pl.ds(0, 2), :] = lat_lo[side]
        xp[side, pl.ds(lats + 2, 2), :] = lat_hi[side]
    hide(0, 2)
    hide(lons, 2)

    step = mine.shape[0] // pieces
    cross = (1 - x) * 2 + s
    copies = []
    for g in range(pieces):
        part_rows = pl.ds(g * step, step)
        copies.append((
            pltpu.make_async_remote_copy(
                mine.at[part_rows], tg.at[part_rows, dev], gb_s.at[g], gb_r.at[g],
                device_id={"ch": 1 - x}, device_id_type=MESH),
            pltpu.make_async_remote_copy(
                mine.at[part_rows], tg.at[part_rows, dev], ga_s.at[g], ga_r.at[g],
                device_id={"sub": 1 - s}, device_id_type=MESH),
            pltpu.make_async_remote_copy(
                tg.at[part_rows, cross], tg.at[part_rows, cross], gf_s.at[g], gf_r.at[g],
                device_id={"sub": 1 - s}, device_id_type=MESH),
        ))
    for g, (over_x, over_s, _) in enumerate(copies):
        count = 2 * step
        field = row_conv(hp, kt2, product, g * count, count, width, chans)
        field = field.astype(jnp.bfloat16).astype(jnp.float32)
        field = field.reshape(step, 2, width, chans)
        fp[...] = jnp.concatenate([field[:, 0], field[:, 1]], axis=2)
        mine[pl.ds(g * step, step)] = jnp.concatenate(
            [fp[:, pl.ds(b, lats // 2, stride=2), :] for b in range(2)], axis=2
        ).astype(jnp.bfloat16)
        over_x.start()
        over_s.start()
    tg[:, dev] = mine[...]
    for over_x, _, onward in copies:
        over_x.wait_recv()
        onward.start()
    for over_x, over_s, onward in copies:
        over_s.wait_recv()
        onward.wait_recv()
        over_x.wait_send()
        over_s.wait_send()
        onward.wait_send()
    for copy in lon_halos:
        copy.wait_send()

    @pl.when(dev < last)
    def _():
        for copy in to_next():
            copy.wait_send()

    @pl.when(dev > 0)
    def _():
        for copy in to_before():
            copy.wait_send()

    flat = tg[...].reshape(tt.shape[1], pet.shape[1])
    tt[...] = lax.dot_general(
        pet[...], flat, (((1,), (1,)), ((), ())), preferred_element_type=jnp.float32
    ).astype(jnp.bfloat16)

    def right_copy(c, d):
        return pltpu.make_async_remote_copy(
            s_r.at[c, d], r_r.at[c, d], rs_s.at[c, d], rs_r.at[c, d],
            device_id={"tok": z + 1}, device_id_type=MESH)

    def left_copy(c, d):
        return pltpu.make_async_remote_copy(
            s_l.at[c, d], r_l.at[c, d], ls_s.at[c, d], ls_r.at[c, d],
            device_id={"tok": z - 1}, device_id_type=MESH)

    def out_copy(c):
        return pltpu.make_async_copy(
            done.at[c], out_ref.at[:, pl.ds(pl.multiple_of(c * hc, hc), hc)], o_sem.at[c]
        )

    def sources(i):
        for d in range(n - 1, 0, -1):
            c = i - (n - 1 - d) * DELAY

            @pl.when((z == 0) & (c >= 0) & (c < chunks))
            def _():
                s_r[c, d] = part[c, d].astype(jnp.bfloat16)
                right_copy(c, d).start()

        for d in range(n - 1):
            c = i - d * DELAY

            @pl.when((z == n - 1) & (c >= 0) & (c < chunks))
            def _():
                s_l[c, d] = part[c, d].astype(jnp.bfloat16)
                left_copy(c, d).start()

    def compute(c, carry):
        w_copy(c).wait()
        product = jnp.dot(tt[...], wv[c], preferred_element_type=jnp.float32)
        part[c] = product.reshape(n, ob, hc)

        sources(c)
        return carry

    lax.fori_loop(0, chunks, compute, 0)
    for late in range((n - 2) * DELAY):
        sources(chunks + late)

    right_lag = jnp.maximum(z - 1, 0) * LAG
    left_lag = jnp.maximum(n - 2 - z, 0) * LAG
    last_lag = jnp.maximum(right_lag + (n - 1 - z) * DELAY, left_lag + z * DELAY)

    def forward(i, carry):
        c_o = i - last_lag
        for d in range(n - 1, 0, -1):
            c_r = i - right_lag - (n - 1 - d) * DELAY

            @pl.when((z > 0) & (z < d) & (c_r >= 0) & (c_r < chunks))
            def _():
                right_copy(c_r, d).wait_recv()
                s_r[c_r, d] = (part[c_r, d] + r_r[c_r, d].astype(jnp.float32)).astype(jnp.bfloat16)
                right_copy(c_r, d).start()

        for d in range(n - 1):
            c_l = i - left_lag - d * DELAY

            @pl.when((z < n - 1) & (z > d) & (c_l >= 0) & (c_l < chunks))
            def _():
                left_copy(c_l, d).wait_recv()
                s_l[c_l, d] = (part[c_l, d] + r_l[c_l, d].astype(jnp.float32)).astype(jnp.bfloat16)
                left_copy(c_l, d).start()

        for d in range(n):
            @pl.when((z == d) & (c_o >= 0) & (c_o < chunks))
            def _():
                total = part[c_o, d]
                if d > 0:
                    right_copy(c_o, d).wait_recv()
                    total = total + r_r[c_o, d].astype(jnp.float32)
                if d < n - 1:
                    left_copy(c_o, d).wait_recv()
                    total = total + r_l[c_o, d].astype(jnp.float32)
                done[c_o] = gelu_exact(total).astype(done.dtype)
                out_copy(c_o).start()

        return carry

    lax.fori_loop(0, chunks + (n - 1) * DELAY + (n - 2) * LAG, forward, 0)

    def drain(c, carry):
        out_copy(c).wait()
        for d in range(n):
            @pl.when(z < d)
            def _():
                right_copy(c, d).wait_send()

            @pl.when(z > d)
            def _():
                left_copy(c, d).wait_send()

        return carry

    lax.fori_loop(0, chunks, drain, 0)


def lift(turned, conv_first, conv_second, patch_embed, token_mixing):
    n = lax.axis_size("tok")
    lons, lats, chans = turned.shape
    embed = patch_embed.shape[1]
    depth, cols = token_mixing.shape
    hc = cols // CHUNKS
    ob = embed // n
    width = lats + 8
    dma, bf16, f32 = pltpu.SemaphoreType.DMA, jnp.bfloat16, jnp.float32
    blocks = pltpu.VMEM((CHUNKS, n, ob, hc), bf16)
    return pl.pallas_call(
        functools.partial(lift_kernel, n),
        out_shape=jax.ShapeDtypeStruct((ob, cols), bf16),
        in_specs=[pl.BlockSpec(memory_space=pl.ANY)] * 5,
        out_specs=pl.BlockSpec(memory_space=pl.ANY),
        scratch_shapes=[
            pltpu.VMEM(turned.shape, f32),
            pltpu.VMEM(conv_first.shape, f32),
            pltpu.VMEM(conv_second.shape, f32),
            pltpu.VMEM(patch_embed.shape, bf16),
            pltpu.VMEM((lons + 5, width, chans), f32),
            pltpu.VMEM(((lons + 3) * width, chans), f32),
            pltpu.VMEM((lons // 2 // PIECES, width, 2 * chans), f32),
            pltpu.VMEM(((lons + 4) * width, 3 * chans), f32),
            pltpu.VMEM((embed // 128, 4 * chans, 128), f32),
            pltpu.VMEM((embed, 4 * chans), bf16),
            pltpu.VMEM((lons, 2, chans), f32),
            pltpu.VMEM((lons, 2, chans), f32),
            pltpu.VMEM((lons + 4, 2, chans), f32),
            pltpu.VMEM((lons + 4, 2, chans), f32),
            pltpu.VMEM((2, lats, chans), f32),
            pltpu.VMEM((2, lats, chans), f32),
            pltpu.VMEM((lons // 2, lats // 2, 4 * chans), bf16),
            pltpu.VMEM((lons // 2, 4, lats // 2, 4 * chans), bf16),
            pltpu.VMEM((embed, depth), bf16),
            pltpu.VMEM((CHUNKS, depth, hc), bf16),
            pltpu.VMEM((CHUNKS, ob, hc), bf16),
            pltpu.VMEM((CHUNKS, n, ob, hc), f32),
            blocks, blocks, blocks, blocks,
            dma((4,)), dma((8,)), dma((8,)), dma((CHUNKS,)), dma((CHUNKS,)),
        ] + [dma((PIECES,))] * 6 + [dma((CHUNKS, n))] * 4,
        compiler_params=pltpu.CompilerParams(
            collective_id=0, has_side_effects=True, vmem_limit_bytes=60 * 1024 * 1024
        ),
    )(turned, conv_first, conv_second, patch_embed, token_mixing)


def fits(weather, token_mixing, embed):
    n = lax.axis_size("tok")
    return (
        lax.axis_size("ch") == 2
        and lax.axis_size("sub") == 2
        and 2 < n <= 8
        and embed % (16 * n) == 0
        and token_mixing.shape[1] % (128 * CHUNKS) == 0
        and weather.shape[1] % (4 * PIECES) == 0
        and weather.shape[2] % 32 == 0
        and 2 * weather.shape[0] == 128
        and embed % 128 == 0
    )


def local(weather, conv_first, conv_second, patch_embed, token_mixing):
    if fits(weather, token_mixing, patch_embed.shape[1]):
        turned = jnp.transpose(weather, (1, 2, 0))
        return lift(turned, conv_first, conv_second, patch_embed, token_mixing)
    widened = padded_2(weather, (("tok", 1),), 2, True)
    padded = padded_2(widened, ((("ch", "sub"), 2),), 2, False)
    hidden_one = jax.nn.gelu(valid_conv(padded, conv_first), approximate=False)
    width_lat = weather.shape[2]
    lat_index = (
        jnp.arange(width_lat + 2, dtype=jnp.int32) - 1 + lax.axis_index(("ch", "sub")) * width_lat
    )
    inside = (lat_index >= 0) & (lat_index < width_lat * lax.axis_size(("ch", "sub")))
    hidden_one = jnp.where(inside[None, None, :], hidden_one, jnp.float32(0.0))
    field_two = valid_conv(hidden_one, conv_second)
    field_two = field_two.astype(jnp.bfloat16)
    local_tokens = embed_patches(field_two, patch_embed)
    gathered = lax.all_gather(local_tokens, ("ch", "sub"), axis=1, tiled=True)
    tokens = gathered.reshape(-1, gathered.shape[2])
    summed = lax.psum_scatter(
        lax.dot_general(
            tokens, token_mixing, (((0,), (0,)), ((), ())), preferred_element_type=jnp.float32
        ),
        "tok",
        scatter_dimension=0,
        tiled=True,
    )
    return jax.nn.gelu(summed, approximate=False).astype(jnp.bfloat16)


def solution(mesh):
    placed = (P("groups", "tok", ("ch", "sub")), P(), P(), P(), P("tok", ("ch", "sub")))
    return jax.shard_map(
        local,
        mesh=mesh,
        in_specs=placed,
        out_specs=P(("groups", "tok"), ("ch", "sub")),
        check_vma=False,
    )
```
